32 devices in a mesh: ka: 2 (over core), pair: 16 (over z, y, x).
Axes of the slice: x: 2, y: 2, z: 4, core: 2. Of those that a mesh axis runs over, the one named last changes fastest.
Arguments:
- cond_orbitals: bfloat16 [2, 2048, 2048], P('ka', 'pair'), may hold values from -6 to 6
- cond_energy: float32 [2, 2048], P('ka', 'pair'), may hold values from 0.5 to 8
- val_orbitals: bfloat16 [32, 2048], P(('ka', 'pair')), may hold values from -6 to 6
- val_energy: bfloat16 [32], P(('ka', 'pair')), may hold values from -8 to -0.5
- val_slots: int32 [2, 16, 16], P('ka', 'pair'), may hold values from 0 to 31
- owner_count: int32 [2, 16], P('ka', 'pair'), may hold values from 1 to 16, as said below
Outputs:
- response: float32 [2, 2048, 512], P('ka', 'pair')
The draws below stay inside these ranges and needn't reach their ends.
Inputs may be any that keep to these rules, and one draw needn't show every extreme that they name: `owner_count`: in every lane some owner has exactly 16 live slots.
All inputs are finite; a program needn't handle non-finite values.
Results may differ from the reference program's by a relative error of at most 0.0047.
The reference program's roundings to bfloat16 on the way count: a program that leaves them out, or rounds other values in their place, can miss the bound.
Values may be sent and summed in bfloat16 or wider, within the bound.
A program may use at most 64 MiB of HBM per device.

```python
import jax
import jax.numpy as jnp
from jax import lax

BC = 128
GA = 16
GB = 128
WIN = 512
SLOTS = 16
GRID = 2048
NC = 2048
NVAL = 32
LANES = 2
N_PAIR = 16


def draw_owner_count(key, part):
    first, second = jax.random.split(key)
    counts = jax.random.randint(first, (LANES, N_PAIR), 1, SLOTS + 1)
    where_full = jax.random.randint(second, (LANES, 1), 0, N_PAIR)
    owners = jnp.arange(N_PAIR, dtype=jnp.int32)[None, :]
    return jnp.where(owners == where_full, SLOTS, counts).astype(jnp.int32)


def touch_ends(array, key, least, largest):
    dims = array.shape
    index_at = [jax.random.randint(jax.random.fold_in(key, axis), (), 0, dims[axis]) for axis in range(len(dims))]
    array = array.at[tuple(index_at)].set(least)
    longest = dims.index(max(dims))
    index_at[longest] = (index_at[longest] + 1) % dims[longest]
    return array.at[tuple(index_at)].set(largest)


def block_scale(key, extent, pieces, smallest, largest):
    level = 1.0
    for position, parts in pieces:
        steps = jax.random.uniform(jax.random.fold_in(jax.random.fold_in(key, 6), position), (parts,), jnp.float32, smallest / len(pieces), largest / len(pieces))
        level = level * jnp.repeat(jnp.exp(steps), extent[position] // parts).reshape((-1,) + (1,) * (len(extent) - 1 - position))
    return level


def normal_values(rng, dims, scale, most, cuts=(), kind=jnp.bfloat16):
    values = jax.random.normal(rng, dims, jnp.float32) * scale
    if len(cuts) > 0:
        values = block_scale(rng, dims, cuts, -0.22, 0.18) * values
    return jnp.clip(values, min=-most, max=most).astype(kind)


def setup_inputs(seed: int = 0) -> dict:
    seeds = jax.random.split(jax.random.key(seed), 7)
    return {
        "cond_orbitals": normal_values(seeds[0], (LANES, GRID, NC), 1.0, 6.0, ((0, 2), (1, 16))),
        "cond_energy": jnp.clip(0.5 + 7.5 * jax.random.uniform(seeds[1], (LANES, NC), jnp.float32) ** block_scale(seeds[1], (LANES, NC), ((0, 2), (1, 16)), -0.2, 0.2), 0.5, 8.0),
        "val_orbitals": normal_values(seeds[2], (NVAL, GRID), 1.0, 6.0, ((0, 32),)),
        "val_energy": jnp.clip(-8.0 + 7.5 * jax.random.uniform(seeds[3], (NVAL,), jnp.float32) ** block_scale(seeds[3], (NVAL,), ((0, 32),), -0.2, 0.2), -8.0, -0.5).astype(jnp.bfloat16),
        "val_slots": touch_ends(jax.random.randint(seeds[4], (LANES, N_PAIR, SLOTS), 0, NVAL), jax.random.fold_in(seeds[4], 1), 0, NVAL - 1).astype(jnp.int32),
        "owner_count": draw_owner_count(jax.random.fold_in(seeds[6], 71), 0),
    }


def cosine_table(length):
    freq = lax.iota(jnp.float32, length)[:, None]
    point = lax.iota(jnp.float32, length)[None, :]
    factor = jnp.where(freq == 0, jnp.sqrt(1.0 / length), jnp.sqrt(2.0 / length))
    return (factor * jnp.cos(jnp.pi * (point + 0.5) * freq / length)).astype(jnp.bfloat16)

def owner_terms(picked, e_pick, live, cond_block, e_cond, table_a, table_b):
    slots = picked.shape[0]
    pair_real = (picked[:, None, :].astype(jnp.float32) * cond_block[None].astype(jnp.float32)).astype(jnp.bfloat16)
    count = slots * cond_block.shape[0]
    rows = pair_real.reshape(count * GA, GB)
    first = jnp.dot(rows, table_b.T, preferred_element_type=jnp.float32).astype(jnp.bfloat16)
    first = first.reshape(count, GA, GB)
    moved = jnp.einsum('ja,pak->pjk', table_a.astype(jnp.float32), first.astype(jnp.float32))
    moved = moved.astype(jnp.bfloat16).reshape(count, GA * GB)
    weight = live[:, None] * 2.0 / (e_cond[None, :] - e_pick[:, None])
    weighted = (moved[:, :WIN].astype(jnp.float32) * weight.reshape(count, 1)).astype(jnp.bfloat16)
    return (moved, weighted)

def reference(cond_orbitals, cond_energy, val_orbitals, val_energy, val_slots, owner_count):
    table_a = cosine_table(GA)
    table_b = cosine_table(GB)
    val_float = val_energy.astype(jnp.float32)

    def one_lane(lane):
        cond_all = cond_orbitals[lane].T.reshape(N_PAIR, BC, GA * GB)
        energy_all = cond_energy[lane].reshape(N_PAIR, BC)

        def add_owner(total, owner):
            slots = val_slots[lane, owner]
            picked = jnp.take(val_orbitals, slots, axis=0)
            e_pick = jnp.take(val_float, slots)
            live = (lax.iota(jnp.int32, SLOTS) < owner_count[lane, owner]).astype(jnp.float32)
            moved, weighted = owner_terms(picked, e_pick, live, cond_all[owner], energy_all[owner], table_a, table_b)
            term = lax.dot_general(moved.astype(jnp.float32), weighted.astype(jnp.float32), (((0,), (0,)), ((), ())))
            return (total + term, None)
        start = jnp.zeros((GA * GB, WIN), jnp.float32)
        total, unused = lax.scan(add_owner, start, jnp.arange(N_PAIR, dtype=jnp.int32))
        return total * (2.0 / (SLOTS * BC * N_PAIR))
    return lax.map(one_lane, jnp.arange(LANES, dtype=jnp.int32))
```

```python
import functools

import jax
import jax.numpy as jnp
import numpy as np
from jax import lax
from jax.experimental import pallas as pl
from jax.experimental.pallas import tpu as pltpu
from jax.sharding import PartitionSpec as P

GA = 16
GB = 128
MESH = pl.DeviceIdType.MESH
F32 = jnp.float32
BF16 = jnp.bfloat16


def cosine_table(length):
    freq = lax.iota(jnp.float32, length)[:, None]
    point = lax.iota(jnp.float32, length)[None, :]
    factor = jnp.where(freq == 0, jnp.sqrt(1.0 / length), jnp.sqrt(2.0 / length))
    return (factor * jnp.cos(jnp.pi * (point + 0.5) * freq / length)).astype(jnp.bfloat16)


def kernel(
    ka_size, n, scale,
    slots_ref, count_ref, ec_ref, msg_ref, tb_ref, t2_ref, cond_ref,
    out_ref,
    vals, cblk, pk, wrow, first, moved, wt,
    part_a, part_b, got1_a, got1_b, send2_a, send2_b, got2_a, got2_b, send3, got3,
    v_send, v_recv, c_send, c_recv, s1, r1, s2, r2, s3, r3,
):
    my_ka = lax.axis_index("ka")
    me = lax.axis_index("pair")
    flat = my_ka * n + me
    devices = ka_size * n
    slots = slots_ref.shape[0]
    bc = ec_ref.shape[1]
    rows = cond_ref.shape[0]
    win = out_ref.shape[1]
    half = win // 2
    groups = n // 4
    per_a = n // GA
    rb = GB // 8

    barrier = pltpu.get_barrier_semaphore()

    def greet(i, carry):
        other = lax.rem(flat + i, devices)
        pl.semaphore_signal(
            barrier, inc=1, device_id=(other // n, lax.rem(other, n)), device_id_type=MESH
        )
        return carry

    lax.fori_loop(1, devices, greet, 0)
    own_val = pltpu.make_async_copy(msg_ref, vals.at[flat], c_send.at[me])
    own_val.start()
    own_cond = pltpu.make_async_copy(
        cond_ref.at[:, pl.ds(pl.multiple_of(me * bc, bc), bc)], cblk.at[me], c_recv.at[me]
    )
    own_cond.start()
    pl.semaphore_wait(barrier, devices - 1)

    def send_val(i, carry):
        other = lax.rem(flat + i, devices)
        pltpu.make_async_remote_copy(
            src_ref=msg_ref, dst_ref=vals.at[flat], send_sem=v_send, recv_sem=v_recv,
            device_id=(other // n, lax.rem(other, n)), device_id_type=MESH,
        ).start()
        return carry

    lax.fori_loop(1, devices, send_val, 0)

    def cond_copy(dest, slot):
        return pltpu.make_async_remote_copy(
            src_ref=cond_ref.at[:, pl.ds(pl.multiple_of(dest * bc, bc), bc)],
            dst_ref=cblk.at[slot], send_sem=c_send.at[dest], recv_sem=c_recv.at[slot],
            device_id=(my_ka, dest), device_id_type=MESH,
        )

    def send_cond(i, carry):
        cond_copy(lax.rem(me + i, n), me).start()
        return carry

    lax.fori_loop(1, n, send_cond, 0)

    own_val.wait()
    rest = vals.at[pl.ds(0, devices - 1)]
    pltpu.make_async_copy(rest, rest, v_recv).wait()

    count = count_ref[0]
    for s in range(slots):
        tile = vals[slots_ref[s]]
        pk[:, s, :] = tile[:GA].astype(F32)
        e_v = tile[GA : GA + 1].astype(F32)
        live = jnp.where(jnp.full((1, bc), s, jnp.int32) < count, 1.0, 0.0)
        wrow[0:1, s * bc : (s + 1) * bc] = live * 2.0 / (ec_ref[...] - e_v)

    my_a = me // per_a

    def do_first(i, carry):
        a = lax.rem(my_a + GA - i, GA)
        for r in range(per_a):
            src = a * per_a + r
            pltpu.make_async_copy(cblk.at[src], cblk.at[src], c_recv.at[src]).wait()
        block = cblk[pl.ds(a * per_a, per_a)].reshape(GB, bc).astype(F32)
        cols = pk[a].T
        for pair in range(slots // 2):
            x = jnp.concatenate(
                [(block * cols[:, s : s + 1]).astype(BF16) for s in (2 * pair, 2 * pair + 1)],
                axis=1,
            )
            f = jnp.dot(tb_ref[...], x, preferred_element_type=F32).astype(BF16)
            for kg in range(8):
                first[
                    kg, pl.ds(pl.multiple_of(a * rb, rb), rb), pair * 2 * bc : (pair + 1) * 2 * bc
                ] = f[kg * rb : (kg + 1) * rb]
        return carry

    lax.fori_loop(0, GA, do_first, 0)

    def do_moved(kg, carry):
        at = pl.multiple_of(kg * rb, rb)
        for pc in range(slots // 2):
            sl = slice(pc * 2 * bc, (pc + 1) * 2 * bc)
            mv = jnp.dot(t2_ref[...], first[kg, :, sl], preferred_element_type=F32).astype(BF16)
            for j in range(GA):
                piece = mv[j * rb : (j + 1) * rb]
                moved[pl.ds(j * GB + at, rb), sl] = piece
                if j * GB < win:
                    wt[pl.ds(j * GB + at, rb), sl] = (
                        piece.astype(F32) * wrow[0:1, sl]
                    ).astype(BF16)
        return carry

    lax.fori_loop(0, 8, do_moved, 0)

    mz = me // 4
    my = lax.rem(me, 4) // 2
    mx = lax.rem(me, 2)
    px, py = 1 - mx, 1 - my
    x_peer = mz * 4 + my * 2 + px
    y_peer = mz * 4 + py * 2 + mx

    def remote(src, dst, ssem, rsem, dest):
        return pltpu.make_async_remote_copy(
            src_ref=src, dst_ref=dst, send_sem=ssem, recv_sem=rsem,
            device_id=(my_ka, dest), device_id_type=MESH,
        )

    def step1(t):
        return (
            remote(part_a.at[px, t], got1_a.at[t], s1.at[0, t], r1.at[0, t], x_peer),
            remote(part_b.at[py, t], got1_b.at[t], s1.at[1, t], r1.at[1, t], y_peer),
        )

    def step2(t):
        return (
            remote(send2_a.at[t], got2_a.at[t], s2.at[0, t], r2.at[0, t], y_peer),
            remote(send2_b.at[t], got2_b.at[t], s2.at[1, t], r2.at[1, t], x_peer),
        )

    def step3(t):
        dest = lax.rem(mz + 1 + t, groups) * 4 + my * 2 + mx
        return remote(send3.at[t], got3.at[t], s3.at[t], r3.at[t], dest)

    def both(t):
        a = part_a[mx, t, my].astype(F32) + got1_a[t, my].astype(F32) + got2_a[t].astype(F32)
        b = part_b[my, t, mx].astype(F32) + got1_b[t, mx].astype(F32) + got2_b[t].astype(F32)
        return a, b

    def flow(i, carry):
        @pl.when(i < groups)
        def _():
            t = i
            z = lax.rem(mz + 1 + t, groups)
            lhs = moved[pl.ds(pl.multiple_of(z * 4 * rows, 4 * rows), 4 * rows), :]
            for h in range(2):
                acc = lax.dot_general(
                    lhs, wt[h * half : (h + 1) * half, :], (((1,), (1,)), ((), ())),
                    preferred_element_type=F32,
                ).astype(BF16)
                for y in range(2):
                    for x in range(2):
                        piece = acc[(2 * y + x) * rows : (2 * y + x + 1) * rows]
                        if h == 0:
                            part_a[x, t, y] = piece
                        else:
                            part_b[y, t, x] = piece
                step1(t)[h].start()

        @pl.when((i >= 2) & (i < groups + 2))
        def _():
            t = i - 2
            first_a, first_b = step1(t)
            second_a, second_b = step2(t)
            first_a.wait_recv()
            send2_a[t] = (part_a[mx, t, py].astype(F32) + got1_a[t, py].astype(F32)).astype(BF16)
            second_a.start()
            first_b.wait_recv()
            send2_b[t] = (part_b[my, t, px].astype(F32) + got1_b[t, px].astype(F32)).astype(BF16)
            second_b.start()

        @pl.when((i >= 4) & (i < groups + 3))
        def _():
            t = i - 4
            for copy in step2(t):
                copy.wait_recv()
            a, b = both(t)
            send3[t, :, :half] = a.astype(BF16)
            send3[t, :, half:] = b.astype(BF16)
            step3(t).start()

        return carry

    lax.fori_loop(0, groups + 3, flow, 0)

    last = groups - 1
    for copy in step2(last):
        copy.wait_recv()
    a, b = both(last)
    for t in range(groups - 1):
        step3(t).wait_recv()
        a = a + got3[t, :, :half].astype(F32)
        b = b + got3[t, :, half:].astype(F32)
    out_ref[:, :half] = a * scale
    out_ref[:, half:] = b * scale

    pltpu.make_async_copy(rest, rest, v_send).wait()

    def drain_cond(i, carry):
        cond_copy(lax.rem(me + i, n), me).wait_send()
        return carry

    lax.fori_loop(1, n, drain_cond, 0)

    def drain(t, carry):
        for copy in step1(t) + step2(t):
            copy.wait_send()
        return carry

    lax.fori_loop(0, groups, drain, 0)
    for t in range(groups - 1):
        step3(t).wait_send()


def shards(ka_size, n, cond_orbitals, cond_energy, val_orbitals, val_energy, val_slots, owner_count):
    cond = cond_orbitals[0]
    rows, bc = cond.shape[0], cond.shape[1] // n
    slots = val_slots.shape[2]
    win = 4 * GB
    half = win // 2
    grid = GA * GB
    count = slots * bc
    groups = n // 4
    msg = jnp.concatenate(
        [val_orbitals.reshape(GA, GB), jnp.broadcast_to(val_energy[:, None], (GA, GB))], axis=0
    )
    table_b = cosine_table(GB)
    rb = GB // 8
    table_2 = (
        cosine_table(GA)[:, None, :, None] * jnp.eye(rb, dtype=BF16)[None, :, None, :]
    ).reshape(GA * rb, GA * rb)
    scale = 2.0 / (slots * bc * n)
    vmem = pl.BlockSpec(memory_space=pltpu.VMEM)
    smem = pl.BlockSpec(memory_space=pltpu.SMEM)
    dma = pltpu.SemaphoreType.DMA
    out = pl.pallas_call(
        functools.partial(kernel, ka_size, n, scale),
        out_shape=jax.ShapeDtypeStruct((rows, win), F32),
        in_specs=[smem, smem, vmem, vmem, vmem, vmem, pl.BlockSpec(memory_space=pl.ANY)],
        out_specs=vmem,
        scratch_shapes=[
            pltpu.VMEM((ka_size * n, 2 * GA, GB), BF16),
            pltpu.VMEM((n, rows, bc), BF16),
            pltpu.VMEM((GA, slots, GB), F32),
            pltpu.VMEM((8, count), F32),
            pltpu.VMEM((8, GA * rb, count), BF16),
            pltpu.VMEM((grid, count), BF16),
            pltpu.VMEM((win, count), BF16),
            pltpu.VMEM((2, groups, 2, rows, half), BF16),
            pltpu.VMEM((2, groups, 2, rows, half), BF16),
            pltpu.VMEM((groups, 2, rows, half), BF16),
            pltpu.VMEM((groups, 2, rows, half), BF16),
            pltpu.VMEM((groups, rows, half), BF16),
            pltpu.VMEM((groups, rows, half), BF16),
            pltpu.VMEM((groups, rows, half), BF16),
            pltpu.VMEM((groups, rows, half), BF16),
            pltpu.VMEM((groups, rows, win), BF16),
            pltpu.VMEM((groups, rows, win), BF16),
            dma(()), dma(()), dma((n,)), dma((n,)),
            dma((2, groups)), dma((2, groups)), dma((2, groups)), dma((2, groups)),
            dma((groups,)), dma((groups,)),
        ],
        compiler_params=pltpu.CompilerParams(
            collective_id=0, has_side_effects=True, vmem_limit_bytes=60 * 1024 * 1024
        ),
        name="polarizability",
    )(val_slots[0, 0], owner_count[0], cond_energy, msg, table_b, table_2, cond)
    return out[None]


def solution(mesh):
    return jax.shard_map(
        functools.partial(shards, mesh.shape["ka"], mesh.shape["pair"]),
        mesh=mesh,
        in_specs=(
            P("ka", "pair", None),
            P("ka", "pair"),
            P(("ka", "pair"), None),
            P(("ka", "pair")),
            P("ka", "pair", None),
            P("ka", "pair"),
        ),
        out_specs=P("ka", "pair", None),
        check_vma=False,
    )
```

```python
import functools

import jax
import jax.numpy as jnp
import numpy as np
from jax import lax
from jax.experimental import pallas as pl
from jax.experimental.pallas import tpu as pltpu
from jax.sharding import PartitionSpec as P

GA = 16
GB = 128
LAGS = (2, 4)
MESH = pl.DeviceIdType.MESH
F32 = jnp.float32
BF16 = jnp.bfloat16


def cosine_table(length):
    freq = np.arange(length, dtype=np.float32)[:, None]
    point = np.arange(length, dtype=np.float32)[None, :]
    factor = np.where(freq == 0, np.sqrt(np.float32(1.0 / length)), np.sqrt(np.float32(2.0 / length)))
    angle = np.float32(np.pi) * (point + np.float32(0.5)) * freq / np.float32(length)
    return (factor * np.cos(angle)).astype(jnp.bfloat16)


def xor(value, other):
    out = 0
    for bit in (1, 2, 4, 8, 16, 32, 64, 128):
        out = out + lax.rem(value // bit + other // bit, 2) * bit
    return out


def kernel(
    ka_size, n, scale,
    slots_ref, count_ref, ec_ref, msg_ref, tb_ref, t2_ref, cond_ref,
    out_ref,
    vals, cblk, pk, wrow, first, moved, wt,
    part_a, part_b, got1_a, got1_b, send2_a, send2_b, got2_a, got2_b, send3, got3,
    v_own, v_send, v_recv, l_send, l_recv, c_send, c_recv, s1, r1, s2, r2, s3, r3,
):
    my_ka = lax.axis_index("ka")
    me = lax.axis_index("pair")
    slots = slots_ref.shape[0]
    bc = ec_ref.shape[1]
    rows = cond_ref.shape[0]
    win = out_ref.shape[1]
    half = win // 2
    groups = n // 4
    per_a = n // GA
    rb = GB // 8

    barrier = pltpu.get_barrier_semaphore()

    def greet(c, carry):
        pl.semaphore_signal(barrier, inc=1, device_id=(my_ka, xor(me, c)), device_id_type=MESH)
        return carry

    def greet_core(c, carry):
        pl.semaphore_signal(
            barrier, inc=1, device_id=(lax.rem(my_ka + c, ka_size), me), device_id_type=MESH
        )
        return carry

    lax.fori_loop(1, n, greet, 0)
    lax.fori_loop(1, ka_size, greet_core, 0)
    own_val = pltpu.make_async_copy(msg_ref, vals.at[my_ka, me], v_own)
    own_val.start()
    own_cond = pltpu.make_async_copy(
        cond_ref.at[:, pl.ds(pl.multiple_of(me * bc, bc), bc)], cblk.at[me], c_recv.at[me]
    )
    own_cond.start()
    pl.semaphore_wait(barrier, n + ka_size - 2)

    def send_val(c, carry):
        pltpu.make_async_remote_copy(
            src_ref=msg_ref, dst_ref=vals.at[my_ka, me], send_sem=v_send, recv_sem=v_recv,
            device_id=(my_ka, xor(me, c)), device_id_type=MESH,
        ).start()
        return carry

    lax.fori_loop(1, n, send_val, 0)

    def cond_copy(dest, slot):
        return pltpu.make_async_remote_copy(
            src_ref=cond_ref.at[:, pl.ds(pl.multiple_of(dest * bc, bc), bc)],
            dst_ref=cblk.at[slot], send_sem=c_send.at[dest], recv_sem=c_recv.at[slot],
            device_id=(my_ka, dest), device_id_type=MESH,
        )

    def send_cond(c, carry):
        cond_copy(xor(me, c), me).start()
        return carry

    lax.fori_loop(1, 4, send_cond, 0)
    lax.fori_loop(n // 2, n, send_cond, 0)
    lax.fori_loop(4, n // 2, send_cond, 0)

    own_val.wait()
    rest = vals.at[my_ka, pl.ds(0, n - 1)]
    pltpu.make_async_copy(rest, rest, v_recv).wait()

    def lane_copy(c):
        other = lax.rem(my_ka + c, ka_size)
        return pltpu.make_async_remote_copy(
            src_ref=vals.at[my_ka], dst_ref=vals.at[my_ka],
            send_sem=l_send.at[other], recv_sem=l_recv.at[my_ka],
            device_id=(other, me), device_id_type=MESH,
        )

    def send_lane(c, carry):
        lane_copy(c).start()
        return carry

    def wait_lane(c, carry):
        other = lax.rem(my_ka + c, ka_size)
        pltpu.make_async_copy(vals.at[other], vals.at[other], l_recv.at[other]).wait()
        return carry

    lax.fori_loop(1, ka_size, send_lane, 0)
    lax.fori_loop(1, ka_size, wait_lane, 0)

    count = count_ref[0]
    for s in range(slots):
        tile = vals[slots_ref[s] // n, lax.rem(slots_ref[s], n)]
        pk[:, s, :] = tile[:GA].astype(F32)
        e_v = tile[GA : GA + 1].astype(F32)
        live = jnp.where(jnp.full((1, bc), s, jnp.int32) < count, 1.0, 0.0)
        wrow[0:1, s * bc : (s + 1) * bc] = live * 2.0 / (ec_ref[...] - e_v)

    my_a = me // per_a

    def do_first(i, carry):
        a = xor(my_a, i)
        for r in range(per_a):
            src = a * per_a + r
            pltpu.make_async_copy(cblk.at[src], cblk.at[src], c_recv.at[src]).wait()
        block = cblk[pl.ds(a * per_a, per_a)].reshape(GB, bc).astype(F32)
        cols = pk[a].T
        for pair in range(slots // 2):
            x = jnp.concatenate(
                [(block * cols[:, s : s + 1]).astype(BF16) for s in (2 * pair, 2 * pair + 1)],
                axis=1,
            )
            f = jnp.dot(tb_ref[...], x, preferred_element_type=F32).astype(BF16)
            for kg in range(8):
                first[
                    kg, pl.ds(pl.multiple_of(a * rb, rb), rb), pair * 2 * bc : (pair + 1) * 2 * bc
                ] = f[kg * rb : (kg + 1) * rb]
        return carry

    lax.fori_loop(0, GA // 4, do_first, 0)
    lax.fori_loop(GA // 2, 3 * GA // 4, do_first, 0)
    lax.fori_loop(GA // 4, GA // 2, do_first, 0)
    lax.fori_loop(3 * GA // 4, GA, do_first, 0)

    def do_moved(kg, carry):
        at = pl.multiple_of(kg * rb, rb)
        for pc in range(slots // 2):
            sl = slice(pc * 2 * bc, (pc + 1) * 2 * bc)
            mv = jnp.dot(t2_ref[...], first[kg, :, sl], preferred_element_type=F32).astype(BF16)
            for j in range(GA):
                piece = mv[j * rb : (j + 1) * rb]
                moved[pl.ds(j * GB + at, rb), sl] = piece
                if j * GB < win:
                    wt[pl.ds(j * GB + at, rb), sl] = (
                        piece.astype(F32) * wrow[0:1, sl]
                    ).astype(BF16)
        return carry

    lax.fori_loop(0, 8, do_moved, 0)

    mz = me // 4
    my = lax.rem(me, 4) // 2
    mx = lax.rem(me, 2)
    px, py = 1 - mx, 1 - my
    x_peer = mz * 4 + my * 2 + px
    y_peer = mz * 4 + py * 2 + mx

    def remote(src, dst, ssem, rsem, dest):
        return pltpu.make_async_remote_copy(
            src_ref=src, dst_ref=dst, send_sem=ssem, recv_sem=rsem,
            device_id=(my_ka, dest), device_id_type=MESH,
        )

    def step1(t):
        return (
            remote(part_a.at[px, t], got1_a.at[t], s1.at[0, t], r1.at[0, t], x_peer),
            remote(part_b.at[py, t], got1_b.at[t], s1.at[1, t], r1.at[1, t], y_peer),
        )

    def step2(t):
        return (
            remote(send2_a.at[t], got2_a.at[t], s2.at[0, t], r2.at[0, t], y_peer),
            remote(send2_b.at[t], got2_b.at[t], s2.at[1, t], r2.at[1, t], x_peer),
        )

    def step3(t):
        dest = lax.rem(mz + 1 + t // 2, groups) * 4 + my * 2 + mx
        return remote(send3.at[t], got3.at[t], s3.at[t], r3.at[t], dest)

    def both(t):
        a = part_a[mx, t, my].astype(F32) + got1_a[t, my].astype(F32) + got2_a[t].astype(F32)
        b = part_b[my, t, mx].astype(F32) + got1_b[t, mx].astype(F32) + got2_b[t].astype(F32)
        return a, b

    chunks = 2 * groups
    far = chunks - 2
    lag2, lag3 = LAGS

    def flow(i, carry):
        @pl.when(i < chunks)
        def _():
            t = i
            z = lax.rem(mz + 1 + t // 2, groups)
            col = pl.multiple_of(lax.rem(t, 2) * half, half)
            acc = lax.dot_general(
                moved[pl.ds(pl.multiple_of(z * 4 * rows, 4 * rows), 4 * rows), :],
                wt[pl.ds(col, half), :], (((1,), (1,)), ((), ())),
                preferred_element_type=F32,
            ).astype(BF16)
            for y in range(2):
                for x in range(2):
                    piece = acc[(2 * y + x) * rows : (2 * y + x + 1) * rows]
                    part_a[x, t, y] = piece[:, : half // 2]
                    part_b[y, t, x] = piece[:, half // 2 :]
            for copy in step1(t):
                copy.start()

        @pl.when((i >= lag2) & (i < chunks + lag2))
        def _():
            t = i - lag2
            first_a, first_b = step1(t)
            second_a, second_b = step2(t)
            first_a.wait_recv()
            send2_a[t] = (part_a[mx, t, py].astype(F32) + got1_a[t, py].astype(F32)).astype(BF16)
            second_a.start()
            first_b.wait_recv()
            send2_b[t] = (part_b[my, t, px].astype(F32) + got1_b[t, px].astype(F32)).astype(BF16)
            second_b.start()

        @pl.when((i >= lag3) & (i < far + lag3))
        def _():
            t = i - lag3
            for copy in step2(t):
                copy.wait_recv()
            a, b = both(t)
            send3[t, :, : half // 2] = a.astype(BF16)
            send3[t, :, half // 2 :] = b.astype(BF16)
            step3(t).start()

        return carry

    lax.fori_loop(0, max(chunks + lag2, far + lag3), flow, 0)

    for h in range(2):
        for copy in step2(far + h):
            copy.wait_recv()
        a, b = both(far + h)
        for t in range(h, far, 2):
            step3(t).wait_recv()
            a = a + got3[t, :, : half // 2].astype(F32)
            b = b + got3[t, :, half // 2 :].astype(F32)
        out_ref[:, h * half : h * half + half // 2] = a * scale
        out_ref[:, h * half + half // 2 : (h + 1) * half] = b * scale

    pltpu.make_async_copy(rest, rest, v_send).wait()

    def drain_cond(c, carry):
        cond_copy(xor(me, c), me).wait_send()
        return carry

    lax.fori_loop(1, n, drain_cond, 0)

    def drain(t, carry):
        for copy in step1(t) + step2(t):
            copy.wait_send()
        return carry

    def drain_lane(c, carry):
        lane_copy(c).wait_send()
        return carry

    lax.fori_loop(1, ka_size, drain_lane, 0)
    lax.fori_loop(0, chunks, drain, 0)
    for t in range(far):
        step3(t).wait_send()


def shards(ka_size, n, cond_orbitals, cond_energy, val_orbitals, val_energy, val_slots, owner_count):
    cond = cond_orbitals[0]
    rows, bc = cond.shape[0], cond.shape[1] // n
    slots = val_slots.shape[2]
    win = 4 * GB
    half = win // 2
    grid = GA * GB
    count = slots * bc
    chunks = n // 2
    msg = jnp.concatenate(
        [val_orbitals.reshape(GA, GB), jnp.broadcast_to(val_energy[:, None], (8, GB))], axis=0
    )
    table_b = cosine_table(GB)
    rb = GB // 8
    table_2 = np.kron(cosine_table(GA), np.eye(rb, dtype=np.float32)).astype(jnp.bfloat16)
    scale = 2.0 / (slots * bc * n)
    vmem = pl.BlockSpec(memory_space=pltpu.VMEM)
    smem = pl.BlockSpec(memory_space=pltpu.SMEM)
    dma = pltpu.SemaphoreType.DMA
    out = pl.pallas_call(
        functools.partial(kernel, ka_size, n, scale),
        out_shape=jax.ShapeDtypeStruct((rows, win), F32),
        in_specs=[smem, smem, vmem, vmem, vmem, vmem, pl.BlockSpec(memory_space=pl.ANY)],
        out_specs=vmem,
        scratch_shapes=[
            pltpu.VMEM((ka_size, n, GA + 8, GB), BF16),
            pltpu.VMEM((n, rows, bc), BF16),
            pltpu.VMEM((GA, slots, GB), F32),
            pltpu.VMEM((8, count), F32),
            pltpu.VMEM((8, GA * rb, count), BF16),
            pltpu.VMEM((grid, count), BF16),
            pltpu.VMEM((win, count), BF16),
            pltpu.VMEM((2, chunks, 2, rows, half // 2), BF16),
            pltpu.VMEM((2, chunks, 2, rows, half // 2), BF16),
            pltpu.VMEM((chunks, 2, rows, half // 2), BF16),
            pltpu.VMEM((chunks, 2, rows, half // 2), BF16),
            pltpu.VMEM((chunks, rows, half // 2), BF16),
            pltpu.VMEM((chunks, rows, half // 2), BF16),
            pltpu.VMEM((chunks, rows, half // 2), BF16),
            pltpu.VMEM((chunks, rows, half // 2), BF16),
            pltpu.VMEM((chunks, rows, half), BF16),
            pltpu.VMEM((chunks, rows, half), BF16),
            dma(()), dma(()), dma(()), dma((ka_size,)), dma((ka_size,)), dma((n,)), dma((n,)),
            dma((2, chunks)), dma((2, chunks)), dma((2, chunks)), dma((2, chunks)),
            dma((chunks,)), dma((chunks,)),
        ],
        compiler_params=pltpu.CompilerParams(
            collective_id=0, has_side_effects=True, vmem_limit_bytes=60 * 1024 * 1024
        ),
        name="polarizability",
    )(val_slots[0, 0], owner_count[0], cond_energy, msg, jnp.asarray(table_b), jnp.asarray(table_2), cond)
    return out[None]


def solution(mesh):
    return jax.shard_map(
        functools.partial(shards, mesh.shape["ka"], mesh.shape["pair"]),
        mesh=mesh,
        in_specs=(
            P("ka", "pair", None),
            P("ka", "pair"),
            P(("ka", "pair"), None),
            P(("ka", "pair")),
            P("ka", "pair", None),
            P("ka", "pair"),
        ),
        out_specs=P("ka", "pair", None),
        check_vma=False,
    )
```

```python
import functools

import jax
import jax.numpy as jnp
import numpy as np
from jax import lax
from jax.experimental import pallas as pl
from jax.experimental.pallas import tpu as pltpu
from jax.sharding import PartitionSpec as P

GA = 16
GB = 128
LAGS = (2, 4)
MESH = pl.DeviceIdType.MESH
F32 = jnp.float32
BF16 = jnp.bfloat16


def cosine_table(length):
    freq = np.arange(length, dtype=np.float32)[:, None]
    point = np.arange(length, dtype=np.float32)[None, :]
    factor = np.where(freq == 0, np.sqrt(np.float32(1.0 / length)), np.sqrt(np.float32(2.0 / length)))
    angle = np.float32(np.pi) * (point + np.float32(0.5)) * freq / np.float32(length)
    return (factor * np.cos(angle)).astype(jnp.bfloat16)


def xor(value, other):
    out = 0
    for bit in (1, 2, 4, 8, 16, 32, 64, 128):
        out = out + lax.rem(value // bit + other // bit, 2) * bit
    return out


def kernel(
    ka_size, n, scale,
    slots_ref, count_ref, ec_ref, msg_ref, tb_ref, t2_ref, cond_ref,
    out_ref,
    vals, cblk, pk, wrow, first, moved, wt,
    part_a, part_b, got1_a, got1_b, send2_a, send2_b, got2_a, got2_b, send3, got3,
    v_own, v_send, v_recv, l_send, l_recv, c_send, c_recv, s1, r1, s2, r2, s3, r3,
):
    my_ka = lax.axis_index("ka")
    me = lax.axis_index("pair")
    slots = slots_ref.shape[0]
    bc = ec_ref.shape[1]
    rows = cond_ref.shape[0]
    win = out_ref.shape[1]
    half = win // 2
    groups = n // 4
    per_a = n // GA
    rb = GB // 8

    barrier = pltpu.get_barrier_semaphore()

    def greet(c, carry):
        pl.semaphore_signal(barrier, inc=1, device_id=(my_ka, xor(me, c)), device_id_type=MESH)
        return carry

    def greet_core(c, carry):
        pl.semaphore_signal(
            barrier, inc=1, device_id=(lax.rem(my_ka + c, ka_size), me), device_id_type=MESH
        )
        return carry

    lax.fori_loop(1, n, greet, 0)
    lax.fori_loop(1, ka_size, greet_core, 0)
    own_val = pltpu.make_async_copy(msg_ref, vals.at[my_ka, me], v_own)
    own_val.start()
    own_cond = pltpu.make_async_copy(
        cond_ref.at[:, pl.ds(pl.multiple_of(me * bc, bc), bc)], cblk.at[me], c_recv.at[me]
    )
    own_cond.start()
    pl.semaphore_wait(barrier, n + ka_size - 2)

    def send_val(c, carry):
        pltpu.make_async_remote_copy(
            src_ref=msg_ref, dst_ref=vals.at[my_ka, me], send_sem=v_send, recv_sem=v_recv,
            device_id=(my_ka, xor(me, c)), device_id_type=MESH,
        ).start()
        return carry

    lax.fori_loop(1, n, send_val, 0)

    def cond_copy(dest, slot):
        return pltpu.make_async_remote_copy(
            src_ref=cond_ref.at[:, pl.ds(pl.multiple_of(dest * bc, bc), bc)],
            dst_ref=cblk.at[slot], send_sem=c_send.at[dest], recv_sem=c_recv.at[slot],
            device_id=(my_ka, dest), device_id_type=MESH,
        )

    def send_cond(c, carry):
        cond_copy(xor(me, c), me).start()
        return carry

    lax.fori_loop(1, n, send_cond, 0)

    own_val.wait()
    rest = vals.at[my_ka, pl.ds(0, n - 1)]
    pltpu.make_async_copy(rest, rest, v_recv).wait()

    def lane_copy(c):
        other = lax.rem(my_ka + c, ka_size)
        return pltpu.make_async_remote_copy(
            src_ref=vals.at[my_ka], dst_ref=vals.at[my_ka],
            send_sem=l_send.at[other], recv_sem=l_recv.at[my_ka],
            device_id=(other, me), device_id_type=MESH,
        )

    def send_lane(c, carry):
        lane_copy(c).start()
        return carry

    def wait_lane(c, carry):
        other = lax.rem(my_ka + c, ka_size)
        pltpu.make_async_copy(vals.at[other], vals.at[other], l_recv.at[other]).wait()
        return carry

    lax.fori_loop(1, ka_size, send_lane, 0)
    lax.fori_loop(1, ka_size, wait_lane, 0)

    count = count_ref[0]
    for s in range(slots):
        tile = vals[slots_ref[s] // n, lax.rem(slots_ref[s], n)]
        pk[:, s, :] = tile[:GA].astype(F32)
        e_v = tile[GA : GA + 1].astype(F32)
        live = jnp.where(jnp.full((1, bc), s, jnp.int32) < count, 1.0, 0.0)
        wrow[0:1, s * bc : (s + 1) * bc] = live * 2.0 / (ec_ref[...] - e_v)

    my_a = me // per_a

    def do_first(i, carry):
        a = xor(my_a, i)
        for r in range(per_a):
            src = a * per_a + r
            pltpu.make_async_copy(cblk.at[src], cblk.at[src], c_recv.at[src]).wait()
        block = cblk[pl.ds(a * per_a, per_a)].reshape(GB, bc)
        cols = pk[a].T
        for pair in range(slots // 2):
            x = jnp.concatenate(
                [block * jnp.broadcast_to(cols[:, s : s + 1], (GB, bc)).astype(BF16) for s in (2 * pair, 2 * pair + 1)],
                axis=1,
            )
            f = jnp.dot(tb_ref[...], x, preferred_element_type=F32).astype(BF16)
            for kg in range(8):
                first[
                    kg, pl.ds(pl.multiple_of(a * rb, rb), rb), pair * 2 * bc : (pair + 1) * 2 * bc
                ] = f[kg * rb : (kg + 1) * rb]
        return carry

    lax.fori_loop(0, GA, do_first, 0)

    def do_moved(kg, carry):
        at = pl.multiple_of(kg * rb, rb)
        for pc in range(slots // 2):
            sl = slice(pc * 2 * bc, (pc + 1) * 2 * bc)
            mv = jnp.dot(t2_ref[...], first[kg, :, sl], preferred_element_type=F32).astype(BF16)
            for j in range(GA):
                piece = mv[j * rb : (j + 1) * rb]
                moved[pl.ds(j * GB + at, rb), sl] = piece
                if j * GB < win:
                    wt[pl.ds(j * GB + at, rb), sl] = (
                        piece.astype(F32) * wrow[0:1, sl]
                    ).astype(BF16)
        return carry

    lax.fori_loop(0, 8, do_moved, 0)

    mz = me // 4
    my = lax.rem(me, 4) // 2
    mx = lax.rem(me, 2)
    px, py = 1 - mx, 1 - my
    x_peer = mz * 4 + my * 2 + px
    y_peer = mz * 4 + py * 2 + mx

    def remote(src, dst, ssem, rsem, dest):
        return pltpu.make_async_remote_copy(
            src_ref=src, dst_ref=dst, send_sem=ssem, recv_sem=rsem,
            device_id=(my_ka, dest), device_id_type=MESH,
        )

    def step1(t):
        return (
            remote(part_a.at[px, t], got1_a.at[t], s1.at[0, t], r1.at[0, t], x_peer),
            remote(part_b.at[py, t], got1_b.at[t], s1.at[1, t], r1.at[1, t], y_peer),
        )

    def step2(t):
        return (
            remote(send2_a.at[t], got2_a.at[t], s2.at[0, t], r2.at[0, t], y_peer),
            remote(send2_b.at[t], got2_b.at[t], s2.at[1, t], r2.at[1, t], x_peer),
        )

    def step3(t):
        dest = lax.rem(mz + 1 + t // 2, groups) * 4 + my * 2 + mx
        return remote(send3.at[t], got3.at[t], s3.at[t], r3.at[t], dest)

    def both(t):
        a = part_a[mx, t, my].astype(F32) + got1_a[t, my].astype(F32) + got2_a[t].astype(F32)
        b = part_b[my, t, mx].astype(F32) + got1_b[t, mx].astype(F32) + got2_b[t].astype(F32)
        return a, b

    chunks = 2 * groups
    far = chunks - 2
    lag2, lag3 = LAGS

    def flow(i, carry):
        @pl.when(i < chunks)
        def _():
            t = i
            z = lax.rem(mz + 1 + t // 2, groups)
            col = pl.multiple_of(lax.rem(t, 2) * half, half)
            acc = lax.dot_general(
                moved[pl.ds(pl.multiple_of(z * 4 * rows, 4 * rows), 4 * rows), :],
                wt[pl.ds(col, half), :], (((1,), (1,)), ((), ())),
                preferred_element_type=F32,
            ).astype(BF16)
            for y in range(2):
                for x in range(2):
                    piece = acc[(2 * y + x) * rows : (2 * y + x + 1) * rows]
                    part_a[x, t, y] = piece[:, : half // 2]
                    part_b[y, t, x] = piece[:, half // 2 :]
            for copy in step1(t):
                copy.start()

        @pl.when((i >= lag2) & (i < chunks + lag2))
        def _():
            t = i - lag2
            first_a, first_b = step1(t)
            second_a, second_b = step2(t)
            first_a.wait_recv()
            send2_a[t] = (part_a[mx, t, py].astype(F32) + got1_a[t, py].astype(F32)).astype(BF16)
            second_a.start()
            first_b.wait_recv()
            send2_b[t] = (part_b[my, t, px].astype(F32) + got1_b[t, px].astype(F32)).astype(BF16)
            second_b.start()

        @pl.when((i >= lag3) & (i < far + lag3))
        def _():
            t = i - lag3
            for copy in step2(t):
                copy.wait_recv()
            a, b = both(t)
            send3[t, :, : half // 2] = a.astype(BF16)
            send3[t, :, half // 2 :] = b.astype(BF16)
            step3(t).start()

        return carry

    lax.fori_loop(0, max(chunks + lag2, far + lag3), flow, 0)

    for h in range(2):
        for copy in step2(far + h):
            copy.wait_recv()
        a, b = both(far + h)
        for t in range(h, far, 2):
            step3(t).wait_recv()
            a = a + got3[t, :, : half // 2].astype(F32)
            b = b + got3[t, :, half // 2 :].astype(F32)
        out_ref[:, h * half : h * half + half // 2] = a * scale
        out_ref[:, h * half + half // 2 : (h + 1) * half] = b * scale

    pltpu.make_async_copy(rest, rest, v_send).wait()

    def drain_cond(c, carry):
        cond_copy(xor(me, c), me).wait_send()
        return carry

    lax.fori_loop(1, n, drain_cond, 0)

    def drain(t, carry):
        for copy in step1(t) + step2(t):
            copy.wait_send()
        return carry

    def drain_lane(c, carry):
        lane_copy(c).wait_send()
        return carry

    lax.fori_loop(1, ka_size, drain_lane, 0)
    lax.fori_loop(0, chunks, drain, 0)
    for t in range(far):
        step3(t).wait_send()


def shards(ka_size, n, cond_orbitals, cond_energy, val_orbitals, val_energy, val_slots, owner_count):
    cond = cond_orbitals[0]
    rows, bc = cond.shape[0], cond.shape[1] // n
    slots = val_slots.shape[2]
    win = 4 * GB
    half = win // 2
    grid = GA * GB
    count = slots * bc
    chunks = n // 2
    msg = jnp.concatenate(
        [val_orbitals.reshape(GA, GB), jnp.broadcast_to(val_energy[:, None], (8, GB))], axis=0
    )
    table_b = cosine_table(GB)
    rb = GB // 8
    table_2 = np.kron(cosine_table(GA), np.eye(rb, dtype=np.float32)).astype(jnp.bfloat16)
    scale = 2.0 / (slots * bc * n)
    vmem = pl.BlockSpec(memory_space=pltpu.VMEM)
    smem = pl.BlockSpec(memory_space=pltpu.SMEM)
    dma = pltpu.SemaphoreType.DMA
    out = pl.pallas_call(
        functools.partial(kernel, ka_size, n, scale),
        out_shape=jax.ShapeDtypeStruct((rows, win), F32),
        in_specs=[smem, smem, vmem, vmem, vmem, vmem, pl.BlockSpec(memory_space=pl.ANY)],
        out_specs=vmem,
        scratch_shapes=[
            pltpu.VMEM((ka_size, n, GA + 8, GB), BF16),
            pltpu.VMEM((n, rows, bc), BF16),
            pltpu.VMEM((GA, slots, GB), F32),
            pltpu.VMEM((8, count), F32),
            pltpu.VMEM((8, GA * rb, count), BF16),
            pltpu.VMEM((grid, count), BF16),
            pltpu.VMEM((win, count), BF16),
            pltpu.VMEM((2, chunks, 2, rows, half // 2), BF16),
            pltpu.VMEM((2, chunks, 2, rows, half // 2), BF16),
            pltpu.VMEM((chunks, 2, rows, half // 2), BF16),
            pltpu.VMEM((chunks, 2, rows, half // 2), BF16),
            pltpu.VMEM((chunks, rows, half // 2), BF16),
            pltpu.VMEM((chunks, rows, half // 2), BF16),
            pltpu.VMEM((chunks, rows, half // 2), BF16),
            pltpu.VMEM((chunks, rows, half // 2), BF16),
            pltpu.VMEM((chunks, rows, half), BF16),
            pltpu.VMEM((chunks, rows, half), BF16),
            dma(()), dma(()), dma(()), dma((ka_size,)), dma((ka_size,)), dma((n,)), dma((n,)),
            dma((2, chunks)), dma((2, chunks)), dma((2, chunks)), dma((2, chunks)),
            dma((chunks,)), dma((chunks,)),
        ],
        compiler_params=pltpu.CompilerParams(
            collective_id=0, has_side_effects=True, vmem_limit_bytes=60 * 1024 * 1024
        ),
        name="polarizability",
    )(val_slots[0, 0], owner_count[0], cond_energy, msg, jnp.asarray(table_b), jnp.asarray(table_2), cond)
    return out[None]


def solution(mesh):
    return jax.shard_map(
        functools.partial(shards, mesh.shape["ka"], mesh.shape["pair"]),
        mesh=mesh,
        in_specs=(
            P("ka", "pair", None),
            P("ka", "pair"),
            P(("ka", "pair"), None),
            P(("ka", "pair")),
            P("ka", "pair", None),
            P("ka", "pair"),
        ),
        out_specs=P("ka", "pair", None),
        check_vma=False,
    )
```

```python
import functools

import jax
import jax.numpy as jnp
import numpy as np
from jax import lax
from jax.experimental import pallas as pl
from jax.experimental.pallas import tpu as pltpu
from jax.sharding import PartitionSpec as P

GA = 16
GB = 128
LAGS = (2, 4)
MESH = pl.DeviceIdType.MESH
F32 = jnp.float32
BF16 = jnp.bfloat16


def cosine_table(length):
    freq = np.arange(length, dtype=np.float32)[:, None]
    point = np.arange(length, dtype=np.float32)[None, :]
    factor = np.where(freq == 0, np.sqrt(np.float32(1.0 / length)), np.sqrt(np.float32(2.0 / length)))
    angle = np.float32(np.pi) * (point + np.float32(0.5)) * freq / np.float32(length)
    return (factor * np.cos(angle)).astype(jnp.bfloat16)


def xor(value, other):
    out = 0
    for bit in (1, 2, 4, 8, 16, 32, 64, 128):
        out = out + lax.rem(value // bit + other // bit, 2) * bit
    return out


def kernel(
    ka_size, n, scale,
    slots_ref, count_ref, ec_ref, msg_ref, tb_ref, t2_ref, cond_ref,
    out_ref,
    vals, cblk, pk, wrow, first, moved, wt,
    part_a, part_b, got1_a, got1_b, send2_a, send2_b, got2_a, got2_b, send3, got3,
    v_own, v_send, v_recv, l_send, l_recv, c_send, c_recv, s1, r1, s2, r2, s3, r3,
):
    my_ka = lax.axis_index("ka")
    me = lax.axis_index("pair")
    slots = slots_ref.shape[0]
    bc = ec_ref.shape[1]
    rows = cond_ref.shape[0]
    win = out_ref.shape[1]
    half = win // 2
    groups = n // 4
    per_a = n // GA
    rb = GB // 8

    barrier = pltpu.get_barrier_semaphore()

    def greet(c, carry):
        pl.semaphore_signal(barrier, inc=1, device_id=(my_ka, xor(me, c)), device_id_type=MESH)
        return carry

    def greet_core(c, carry):
        pl.semaphore_signal(
            barrier, inc=1, device_id=(lax.rem(my_ka + c, ka_size), me), device_id_type=MESH
        )
        return carry

    lax.fori_loop(1, n, greet, 0)
    lax.fori_loop(1, ka_size, greet_core, 0)
    own_val = pltpu.make_async_copy(msg_ref, vals.at[my_ka, me], v_own)
    own_val.start()
    own_cond = pltpu.make_async_copy(
        cond_ref.at[:, pl.ds(pl.multiple_of(me * bc, bc), bc)], cblk.at[me], c_recv.at[me]
    )
    own_cond.start()
    pl.semaphore_wait(barrier, n + ka_size - 2)

    def send_val(c, carry):
        pltpu.make_async_remote_copy(
            src_ref=msg_ref, dst_ref=vals.at[my_ka, me], send_sem=v_send, recv_sem=v_recv,
            device_id=(my_ka, xor(me, c)), device_id_type=MESH,
        ).start()
        return carry

    lax.fori_loop(1, n, send_val, 0)

    def cond_copy(dest, slot):
        return pltpu.make_async_remote_copy(
            src_ref=cond_ref.at[:, pl.ds(pl.multiple_of(dest * bc, bc), bc)],
            dst_ref=cblk.at[slot], send_sem=c_send.at[dest], recv_sem=c_recv.at[slot],
            device_id=(my_ka, dest), device_id_type=MESH,
        )

    def send_cond(c, carry):
        cond_copy(xor(me, c), me).start()
        return carry

    lax.fori_loop(1, n, send_cond, 0)

    own_val.wait()
    rest = vals.at[my_ka, pl.ds(0, n - 1)]
    pltpu.make_async_copy(rest, rest, v_recv).wait()

    def lane_copy(c):
        other = lax.rem(my_ka + c, ka_size)
        return pltpu.make_async_remote_copy(
            src_ref=vals.at[my_ka], dst_ref=vals.at[my_ka],
            send_sem=l_send.at[other], recv_sem=l_recv.at[my_ka],
            device_id=(other, me), device_id_type=MESH,
        )

    def send_lane(c, carry):
        lane_copy(c).start()
        return carry

    def wait_lane(c, carry):
        other = lax.rem(my_ka + c, ka_size)
        pltpu.make_async_copy(vals.at[other], vals.at[other], l_recv.at[other]).wait()
        return carry

    lax.fori_loop(1, ka_size, send_lane, 0)
    lax.fori_loop(1, ka_size, wait_lane, 0)

    count = count_ref[0]
    for s in range(slots):
        tile = vals[slots_ref[s] // n, lax.rem(slots_ref[s], n)]
        pk[:, s, :] = tile[:GA].astype(F32)
        e_v = tile[GA : GA + 1].astype(F32)
        live = jnp.where(jnp.full((1, bc), s, jnp.int32) < count, 1.0, 0.0)
        wrow[0:1, s * bc : (s + 1) * bc] = live * 2.0 / (ec_ref[...] - e_v)

    my_a = me // per_a

    def do_first(i, carry):
        a = xor(my_a, i)
        for r in range(per_a):
            src = a * per_a + r
            pltpu.make_async_copy(cblk.at[src], cblk.at[src], c_recv.at[src]).wait()
        block = cblk[pl.ds(a * per_a, per_a)].reshape(GB, bc)
        cols = pk[a].T
        for pair in range(slots // 2):
            x = jnp.concatenate(
                [block * jnp.broadcast_to(cols[:, s : s + 1], (GB, bc)).astype(BF16) for s in (2 * pair, 2 * pair + 1)],
                axis=1,
            )
            f = jnp.dot(tb_ref[...], x, preferred_element_type=F32).astype(BF16)
            for kg in range(8):
                first[
                    kg, pl.ds(pl.multiple_of(a * rb, rb), rb), pair * 2 * bc : (pair + 1) * 2 * bc
                ] = f[kg * rb : (kg + 1) * rb]
        return carry

    lax.fori_loop(0, GA, do_first, 0)

    def do_moved(kg, carry):
        at = pl.multiple_of(kg * rb, rb)
        for pc in range(slots // 2):
            sl = slice(pc * 2 * bc, (pc + 1) * 2 * bc)
            mv = jnp.dot(t2_ref[...], first[kg, :, sl], preferred_element_type=F32).astype(BF16)
            for j in range(GA):
                piece = mv[j * rb : (j + 1) * rb]
                moved[pl.ds(j * GB + at, rb), sl] = piece
                if j * GB < win:
                    wt[pl.ds(j * GB + at, rb), sl] = (
                        piece.astype(F32) * wrow[0:1, sl]
                    ).astype(BF16)
        return carry

    lax.fori_loop(0, 8, do_moved, 0)

    mz = me // 4
    my = lax.rem(me, 4) // 2
    mx = lax.rem(me, 2)
    px, py = 1 - mx, 1 - my
    x_peer = mz * 4 + my * 2 + px
    y_peer = mz * 4 + py * 2 + mx

    def remote(src, dst, ssem, rsem, dest):
        return pltpu.make_async_remote_copy(
            src_ref=src, dst_ref=dst, send_sem=ssem, recv_sem=rsem,
            device_id=(my_ka, dest), device_id_type=MESH,
        )

    def step1(t):
        return (
            remote(part_a.at[px, t], got1_a.at[t], s1.at[0, t], r1.at[0, t], x_peer),
            remote(part_b.at[py, t], got1_b.at[t], s1.at[1, t], r1.at[1, t], y_peer),
        )

    def step2(t):
        return (
            remote(send2_a.at[t], got2_a.at[t], s2.at[0, t], r2.at[0, t], y_peer),
            remote(send2_b.at[t], got2_b.at[t], s2.at[1, t], r2.at[1, t], x_peer),
        )

    def step3(t):
        dest = xor(mz, groups - 1 - t // 2) * 4 + my * 2 + mx
        return remote(send3.at[t], got3.at[t], s3.at[t], r3.at[t], dest)

    def both(t):
        a = part_a[mx, t, my].astype(F32) + got1_a[t, my].astype(F32) + got2_a[t].astype(F32)
        b = part_b[my, t, mx].astype(F32) + got1_b[t, mx].astype(F32) + got2_b[t].astype(F32)
        return a, b

    chunks = 2 * groups
    far = chunks - 2
    lag2, lag3 = LAGS

    def flow(i, carry):
        @pl.when(i < chunks)
        def _():
            t = i
            z = xor(mz, groups - 1 - t // 2)
            col = pl.multiple_of(lax.rem(t, 2) * half, half)
            acc = lax.dot_general(
                moved[pl.ds(pl.multiple_of(z * 4 * rows, 4 * rows), 4 * rows), :],
                wt[pl.ds(col, half), :], (((1,), (1,)), ((), ())),
                preferred_element_type=F32,
            ).astype(BF16)
            for y in range(2):
                for x in range(2):
                    piece = acc[(2 * y + x) * rows : (2 * y + x + 1) * rows]
                    part_a[x, t, y] = piece[:, : half // 2]
                    part_b[y, t, x] = piece[:, half // 2 :]
            for copy in step1(t):
                copy.start()

        @pl.when((i >= lag2) & (i < chunks + lag2))
        def _():
            t = i - lag2
            first_a, first_b = step1(t)
            second_a, second_b = step2(t)
            first_a.wait_recv()
            send2_a[t] = (part_a[mx, t, py].astype(F32) + got1_a[t, py].astype(F32)).astype(BF16)
            second_a.start()
            first_b.wait_recv()
            send2_b[t] = (part_b[my, t, px].astype(F32) + got1_b[t, px].astype(F32)).astype(BF16)
            second_b.start()

        @pl.when((i >= lag3) & (i < far + lag3))
        def _():
            t = i - lag3
            for copy in step2(t):
                copy.wait_recv()
            a, b = both(t)
            send3[t, :, : half // 2] = a.astype(BF16)
            send3[t, :, half // 2 :] = b.astype(BF16)
            step3(t).start()

        return carry

    lax.fori_loop(0, max(chunks + lag2, far + lag3), flow, 0)

    for h in range(2):
        for copy in step2(far + h):
            copy.wait_recv()
        a, b = both(far + h)
        for t in range(h, far, 2):
            step3(t).wait_recv()
            a = a + got3[t, :, : half // 2].astype(F32)
            b = b + got3[t, :, half // 2 :].astype(F32)
        out_ref[:, h * half : h * half + half // 2] = a * scale
        out_ref[:, h * half + half // 2 : (h + 1) * half] = b * scale

    pltpu.make_async_copy(rest, rest, v_send).wait()

    def drain_cond(c, carry):
        cond_copy(xor(me, c), me).wait_send()
        return carry

    lax.fori_loop(1, n, drain_cond, 0)

    def drain(t, carry):
        for copy in step1(t) + step2(t):
            copy.wait_send()
        return carry

    def drain_lane(c, carry):
        lane_copy(c).wait_send()
        return carry

    lax.fori_loop(1, ka_size, drain_lane, 0)
    lax.fori_loop(0, chunks, drain, 0)
    for t in range(far):
        step3(t).wait_send()


def shards(ka_size, n, cond_orbitals, cond_energy, val_orbitals, val_energy, val_slots, owner_count):
    cond = cond_orbitals[0]
    rows, bc = cond.shape[0], cond.shape[1] // n
    slots = val_slots.shape[2]
    win = 4 * GB
    half = win // 2
    grid = GA * GB
    count = slots * bc
    chunks = n // 2
    msg = jnp.concatenate(
        [val_orbitals.reshape(GA, GB), jnp.broadcast_to(val_energy[:, None], (8, GB))], axis=0
    )
    table_b = cosine_table(GB)
    rb = GB // 8
    table_2 = np.kron(cosine_table(GA), np.eye(rb, dtype=np.float32)).astype(jnp.bfloat16)
    scale = 2.0 / (slots * bc * n)
    vmem = pl.BlockSpec(memory_space=pltpu.VMEM)
    smem = pl.BlockSpec(memory_space=pltpu.SMEM)
    dma = pltpu.SemaphoreType.DMA
    out = pl.pallas_call(
        functools.partial(kernel, ka_size, n, scale),
        out_shape=jax.ShapeDtypeStruct((rows, win), F32),
        in_specs=[smem, smem, vmem, vmem, vmem, vmem, pl.BlockSpec(memory_space=pl.ANY)],
        out_specs=vmem,
        scratch_shapes=[
            pltpu.VMEM((ka_size, n, GA + 8, GB), BF16),
            pltpu.VMEM((n, rows, bc), BF16),
            pltpu.VMEM((GA, slots, GB), F32),
            pltpu.VMEM((8, count), F32),
            pltpu.VMEM((8, GA * rb, count), BF16),
            pltpu.VMEM((grid, count), BF16),
            pltpu.VMEM((win, count), BF16),
            pltpu.VMEM((2, chunks, 2, rows, half // 2), BF16),
            pltpu.VMEM((2, chunks, 2, rows, half // 2), BF16),
            pltpu.VMEM((chunks, 2, rows, half // 2), BF16),
            pltpu.VMEM((chunks, 2, rows, half // 2), BF16),
            pltpu.VMEM((chunks, rows, half // 2), BF16),
            pltpu.VMEM((chunks, rows, half // 2), BF16),
            pltpu.VMEM((chunks, rows, half // 2), BF16),
            pltpu.VMEM((chunks, rows, half // 2), BF16),
            pltpu.VMEM((chunks, rows, half), BF16),
            pltpu.VMEM((chunks, rows, half), BF16),
            dma(()), dma(()), dma(()), dma((ka_size,)), dma((ka_size,)), dma((n,)), dma((n,)),
            dma((2, chunks)), dma((2, chunks)), dma((2, chunks)), dma((2, chunks)),
            dma((chunks,)), dma((chunks,)),
        ],
        compiler_params=pltpu.CompilerParams(
            collective_id=0, has_side_effects=True, vmem_limit_bytes=60 * 1024 * 1024
        ),
        name="polarizability",
    )(val_slots[0, 0], owner_count[0], cond_energy, msg, jnp.asarray(table_b), jnp.asarray(table_2), cond)
    return out[None]


def solution(mesh):
    return jax.shard_map(
        functools.partial(shards, mesh.shape["ka"], mesh.shape["pair"]),
        mesh=mesh,
        in_specs=(
            P("ka", "pair", None),
            P("ka", "pair"),
            P(("ka", "pair"), None),
            P(("ka", "pair")),
            P("ka", "pair", None),
            P("ka", "pair"),
        ),
        out_specs=P("ka", "pair", None),
        check_vma=False,
    )
```
